256 devices in a mesh: gx: 8 (over x, core), gy: 4 (over y), gz: 8 (over z).
Axes of the slice: x: 4, y: 4, z: 8, core: 2. Of those that a mesh axis runs over, the one named last changes fastest.
Arguments:
- body_local: float32 [3, 16, 8, 32, 128], P(None, 'gx', 'gy', 'gz'), as said below
- charges: float32 [16, 8, 32, 128], P('gx', 'gy', 'gz'), may hold values from -1 to 1
- radii: float32 [16, 8, 32, 128], P('gx', 'gy', 'gz'), may hold values from 0.05 to 0.15
- body_slot: int32 [16, 8, 32, 128], P('gx', 'gy', 'gz'), may hold values from 0 to 647, as said below
- cell_counts: int32 [16, 8, 32], P('gx', 'gy', 'gz'), may hold values from 16 to 128, as said below
- poses: float32 [12, 6144], P(None, ('gx', 'gy', 'gz')), as said below
- mobility: float32 [2, 6144], P(None, ('gx', 'gy', 'gz')), may hold values from 0.5 to 2
- noise: float32 [6, 6144], P(None, ('gx', 'gy', 'gz')), may hold values from -1 to 1
Outputs:
- stepped_poses: float32 [12, 6144], P(None, ('gx', 'gy', 'gz'))
- positions: float32 [3, 16, 8, 32, 128], P(None, 'gx', 'gy', 'gz')
The draws below stay inside these ranges and needn't reach their ends.
Inputs may be any that keep to these rules, and one draw needn't show every extreme that they name: Every atom slot belongs to a body owned by its own device or by one of the devices next to it along each axis, periodically; body_slot = (9 (dx + 1) + 3 (dy + 1) + (dz + 1)) * 24 + k names body k of the device at offset (dx, dy, dz). `cell_counts`: slots 0 to count - 1 of a cell hold atoms; the other slots are empty. `poses`: rows 0 to 8 form a rotation matrix; the centre lies inside the brick of the owner device. `body_local`: R local + t of every slot lies, up to whole periods of the box, inside the slot's cell.
All inputs are finite; a program needn't handle non-finite values.
Results may differ from the reference program's by a relative error of at most 0.0003.
Values sent between devices are 32-bit elements; how exact they have to be, the bound alone decides.
A program may use at most 64 MiB of HBM per device.

```python
import math
import jax
import jax.numpy as jnp
from jax import lax

BRICK_CELLS_X = 2
CY = 2
CZ = 4
NB_DEV = 24
ATOMS_PER_CELL = 128
BOX_CELLS_X = 16
BOX_CELLS_Y = 8
BOX_CELLS_Z = 32
NBODY = 6144
N_GX = 8
N_GY = 4
N_GZ = 8


def body_poses(key):
    quat = jax.random.normal(jax.random.fold_in(key, 11), (4, NBODY), jnp.float32)
    quat = quat / jnp.sqrt(jnp.sum(quat * quat, axis=0))
    qw, qx, qy, qz = (quat[0], quat[1], quat[2], quat[3])
    rotation = jnp.stack([1 - 2 * (qy * qy + qz * qz), 2 * (qx * qy - qz * qw), 2 * (qx * qz + qy * qw), 2 * (qx * qy + qz * qw), 1 - 2 * (qx * qx + qz * qz), 2 * (qy * qz - qx * qw), 2 * (qx * qz - qy * qw), 2 * (qy * qz + qx * qw), 1 - 2 * (qx * qx + qy * qy)])
    count_y = BOX_CELLS_Y // CY
    count_z = BOX_CELLS_Z // CZ
    device = jnp.arange(NBODY, dtype=jnp.int32) // NB_DEV
    brick_x = device // (count_y * count_z)
    brick_y = device // count_z % count_y
    brick_z = device % count_z
    target_slot = jax.random.uniform(jax.random.fold_in(key, 12), (3, NBODY), jnp.float32)
    centre = jnp.stack([(brick_x + target_slot[0]) * BRICK_CELLS_X, (brick_y + target_slot[1]) * CY, (brick_z + target_slot[2]) * CZ])
    return jnp.concatenate([rotation, centre], axis=0).astype(jnp.float32)


def atom_slots(key):
    array_shape = (BOX_CELLS_X, BOX_CELLS_Y, BOX_CELLS_Z, ATOMS_PER_CELL)
    at_home = jax.random.randint(jax.random.fold_in(key, 21), array_shape, 0, 2)
    code = jnp.where(at_home == 1, 13, jax.random.randint(jax.random.fold_in(key, 22), array_shape, 0, 27))
    member = jax.random.randint(jax.random.fold_in(key, 23), array_shape, 0, NB_DEV)
    return (code * NB_DEV + member).astype(jnp.int32)


def draw_poses(key, part):
    return body_poses(key)


def draw_body_slot(key, part):
    return atom_slots(key)


def draw_cell_counts(key, part):
    slot_counts = jax.random.randint(jax.random.fold_in(key, 31), (BOX_CELLS_X, BOX_CELLS_Y, BOX_CELLS_Z), 16, ATOMS_PER_CELL + 1)
    cell_index_x = jnp.arange(BOX_CELLS_X)[:, None, None] % BRICK_CELLS_X == 0
    cell_y = jnp.arange(BOX_CELLS_Y)[None, :, None] % CY == 0
    cell_z = jnp.arange(BOX_CELLS_Z)[None, None, :] % CZ == 0
    return jnp.where(cell_index_x & cell_y & cell_z, ATOMS_PER_CELL, slot_counts).astype(jnp.int32)


def draw_body_local(key, part):
    pose_rows = body_poses(key)
    slots = atom_slots(key)
    count_along_x = BOX_CELLS_X // BRICK_CELLS_X
    count_y = BOX_CELLS_Y // CY
    count_z = BOX_CELLS_Z // CZ
    cell_index_x = jnp.arange(BOX_CELLS_X, dtype=jnp.int32)[:, None, None, None]
    cell_y = jnp.arange(BOX_CELLS_Y, dtype=jnp.int32)[None, :, None, None]
    cell_z = jnp.arange(BOX_CELLS_Z, dtype=jnp.int32)[None, None, :, None]
    code = slots // NB_DEV
    member = slots % NB_DEV
    owner_x = (cell_index_x // BRICK_CELLS_X + code // 9 - 1) % count_along_x
    owner_y = (cell_y // CY + code // 3 % 3 - 1) % count_y
    owner_z = (cell_z // CZ + code % 3 - 1) % count_z
    body_ids = (((owner_x * count_y + owner_y) * count_z + owner_z) * NB_DEV + member).reshape(-1)
    target_slot = jax.random.uniform(jax.random.fold_in(key, 41), (3, BOX_CELLS_X, BOX_CELLS_Y, BOX_CELLS_Z, ATOMS_PER_CELL), jnp.float32)
    zero_buffer = jnp.zeros((BOX_CELLS_X, BOX_CELLS_Y, BOX_CELLS_Z, ATOMS_PER_CELL), jnp.float32)
    target = jnp.stack([cell_index_x + zero_buffer, cell_y + zero_buffer, cell_z + zero_buffer]) + target_slot
    chosen = jnp.take(pose_rows, body_ids, axis=1)
    delta = target.reshape(3, -1) - chosen[9:12]
    domain_extent = jnp.array([BOX_CELLS_X, BOX_CELLS_Y, BOX_CELLS_Z], jnp.float32)[:, None]
    delta = delta - domain_extent * jnp.floor(delta / domain_extent + 0.5)
    resident_rows = jnp.stack([chosen[col_at] * delta[0] + chosen[3 + col_at] * delta[1] + chosen[6 + col_at] * delta[2] for col_at in range(3)])
    return resident_rows.reshape(3, BOX_CELLS_X, BOX_CELLS_Y, BOX_CELLS_Z, ATOMS_PER_CELL).astype(jnp.float32)


def block_scale(rng, shape, cuts, smallest, largest):
    level, own = 1.0, jax.random.fold_in(rng, 6)
    for position, blocks in cuts:
        heights = jnp.exp(jax.random.uniform(jax.random.fold_in(own, position), (blocks,), jnp.float32, smallest / len(cuts), largest / len(cuts)))
        level = level * jnp.repeat(heights, shape[position] // blocks).reshape([-1 if axis == position else 1 for axis in range(len(shape))])
    return level


def normal_values(stream_key, extent, spread, limit, split=(), held_as=jnp.bfloat16):
    values = spread * jax.random.normal(stream_key, extent, jnp.float32)
    if split:
        values = values * block_scale(stream_key, extent, split, -0.22, 0.18)
    return jnp.clip(values, -limit, limit).astype(held_as)


def setup_inputs(seed: int = 0) -> dict:
    arg_keys = jax.random.split(jax.random.key(seed), 9)
    body_local = draw_body_local(jax.random.fold_in(arg_keys[8], 71), 0)
    charges = jnp.clip(jax.random.uniform(arg_keys[1], (BOX_CELLS_X, BOX_CELLS_Y, BOX_CELLS_Z, ATOMS_PER_CELL), jnp.float32, -1.0, 1.0) * block_scale(arg_keys[1], (BOX_CELLS_X, BOX_CELLS_Y, BOX_CELLS_Z, ATOMS_PER_CELL), ((0, 8), (1, 4), (2, 8)), -0.4, 0.0), -1.0, 1.0)
    radii = jnp.clip(jnp.exp(math.log(0.15) - 1.0986123 * jax.random.uniform(arg_keys[2], (BOX_CELLS_X, BOX_CELLS_Y, BOX_CELLS_Z, ATOMS_PER_CELL), jnp.float32) ** block_scale(arg_keys[2], (BOX_CELLS_X, BOX_CELLS_Y, BOX_CELLS_Z, ATOMS_PER_CELL), ((0, 8), (1, 4), (2, 8)), -0.2, 0.2)), 0.05, 0.15)
    body_slot = draw_body_slot(jax.random.fold_in(arg_keys[8], 71), 0)
    cell_counts = draw_cell_counts(jax.random.fold_in(arg_keys[8], 71), 0)
    poses = draw_poses(jax.random.fold_in(arg_keys[8], 71), 0)
    mobility = jnp.clip(jnp.exp(math.log(2.0) - 1.3862944 * jax.random.uniform(arg_keys[6], (2, NBODY), jnp.float32) ** block_scale(arg_keys[6], (2, NBODY), ((1, 256),), -0.2, 0.2)), 0.5, 2.0)
    noise = normal_values(arg_keys[7], (6, NBODY), 0.2, 1.0, ((1, 256),), jnp.float32)
    return dict(body_local=body_local, charges=charges, radii=radii, body_slot=body_slot, cell_counts=cell_counts, poses=poses, mobility=mobility, noise=noise)


min_reach = 0.15
clash_gain = 20.0
debye_length = 0.5
move_gain = 0.02
turn_gain = 0.01

def pair_force(own_cells, other_cells, domain_extent):
    delta = own_cells[0:3, :, :, None] - other_cells[0:3, :, None, :]
    delta = delta - domain_extent * jnp.floor(delta / domain_extent + 0.5)
    dist_sq = lax.optimization_barrier(jnp.sum(delta * delta, axis=0))
    dist = jnp.sqrt(dist_sq)
    reach = jnp.maximum(dist, min_reach)
    switch = jnp.square(jnp.maximum(1.0 - dist_sq, 0.0))
    sigma = own_cells[4][:, :, None] + other_cells[4][:, None, :]
    clash = clash_gain * jnp.maximum(sigma - dist, 0.0)
    screened = own_cells[3][:, :, None] * other_cells[3][:, None, :] * jnp.exp(-dist / debye_length) * (1.0 / reach + 1.0 / debye_length) / reach * switch
    weight = own_cells[5][:, :, None] * other_cells[5][:, None, :] * (clash + screened) / reach
    return lax.optimization_barrier(jnp.sum(weight[None] * delta, axis=-1))

def place_atoms(pose_rows, resident_rows):
    arm_rows = jnp.stack([pose_rows[3 * row_at] * resident_rows[0] + pose_rows[3 * row_at + 1] * resident_rows[1] + pose_rows[3 * row_at + 2] * resident_rows[2] for row_at in range(3)])
    return (arm_rows, arm_rows + pose_rows[9:12])

def cross_rows(first_rows, second_rows):
    return jnp.stack([first_rows[1] * second_rows[2] - first_rows[2] * second_rows[1], first_rows[2] * second_rows[0] - first_rows[0] * second_rows[2], first_rows[0] * second_rows[1] - first_rows[1] * second_rows[0]])

def advance(pose_rows, totals, mobility, noise):
    centre = pose_rows[9:12] + move_gain * mobility[0] * totals[0:3] + noise[0:3]
    spin = 0.5 * (turn_gain * mobility[1] * totals[3:6] + noise[3:6])
    spin_sq = lax.optimization_barrier(jnp.sum(spin * spin, axis=0))
    factor = 2.0 / (1.0 + spin_sq)
    skew_mat = [[None, -spin[2], spin[1]], [spin[2], None, -spin[0]], [-spin[1], spin[0], None]]
    turn = []
    for row_at in range(3):
        line = []
        for col_at in range(3):
            inner = spin[row_at] * spin[col_at]
            if row_at == col_at:
                line.append(1.0 + factor * (inner - spin_sq))
            else:
                line.append(factor * (skew_mat[row_at][col_at] + inner))
        turn.append(line)
    rotated = []
    for row_at in range(3):
        for col_at in range(3):
            rotated.append(turn[row_at][0] * pose_rows[col_at] + turn[row_at][1] * pose_rows[3 + col_at] + turn[row_at][2] * pose_rows[6 + col_at])
    return jnp.concatenate([jnp.stack(rotated), centre], axis=0)

def owner_ids(body_slot):
    cell_index_x = jnp.arange(BOX_CELLS_X, dtype=jnp.int32)[:, None, None, None]
    cell_y = jnp.arange(BOX_CELLS_Y, dtype=jnp.int32)[None, :, None, None]
    cell_z = jnp.arange(BOX_CELLS_Z, dtype=jnp.int32)[None, None, :, None]
    code = body_slot // NB_DEV
    member = body_slot % NB_DEV
    owner_x = (cell_index_x // BRICK_CELLS_X + code // 9 - 1) % N_GX
    owner_y = (cell_y // CY + code // 3 % 3 - 1) % N_GY
    owner_z = (cell_z // CZ + code % 3 - 1) % N_GZ
    return (((owner_x * N_GY + owner_y) * N_GZ + owner_z) * NB_DEV + member).astype(jnp.int32)

def reference(body_local, charges, radii, body_slot, cell_counts, poses, mobility, noise):
    body_ids = owner_ids(body_slot).reshape(-1)
    resident_rows = body_local.reshape(3, -1)
    arm_rows, placement_index = place_atoms(jnp.take(poses, body_ids, axis=1), resident_rows)
    slot_iota = jnp.arange(ATOMS_PER_CELL, dtype=jnp.int32)[None, None, None, :]
    filled_slots = (slot_iota < cell_counts[..., None]).astype(charges.dtype)
    message_rows = jnp.concatenate([placement_index.reshape(3, BOX_CELLS_X, BOX_CELLS_Y, BOX_CELLS_Z, ATOMS_PER_CELL), charges[None], radii[None], filled_slots[None]], axis=0)
    domain_extent = jnp.array([BOX_CELLS_X, BOX_CELLS_Y, BOX_CELLS_Z], dtype=message_rows.dtype)[:, None, None, None]
    flattened_owned = jnp.moveaxis(message_rows, 1, 0).reshape(BOX_CELLS_X, 6, BOX_CELLS_Y * BOX_CELLS_Z, ATOMS_PER_CELL)

    def visit(running, offset_code):
        step_x = offset_code // 9 - 1
        step_y = offset_code // 3 % 3 - 1
        step_z = offset_code % 3 - 1
        neighbour_block = jnp.roll(message_rows, (-step_x, -step_y, -step_z), axis=(1, 2, 3))
        flattened_neighbour = jnp.moveaxis(neighbour_block, 1, 0).reshape(BOX_CELLS_X, 6, BOX_CELLS_Y * BOX_CELLS_Z, ATOMS_PER_CELL)
        part_force = lax.map(lambda pair: pair_force(pair[0], pair[1], domain_extent), (flattened_owned, flattened_neighbour))
        return (running + part_force, None)
    start_offset = jnp.zeros((BOX_CELLS_X, 3, BOX_CELLS_Y * BOX_CELLS_Z, ATOMS_PER_CELL), message_rows.dtype)
    force_rows = lax.scan(visit, start_offset, jnp.arange(27, dtype=jnp.int32))[0]
    force = jnp.moveaxis(force_rows, 1, 0).reshape(3, -1)
    torque = cross_rows(arm_rows, force)
    contrib = jnp.concatenate([force, torque], axis=0)
    totals = jax.ops.segment_sum(contrib.T, body_ids, num_segments=NBODY).T
    stepped_poses = advance(poses, totals, mobility, noise)
    moved_arm, shifted_poses = place_atoms(jnp.take(stepped_poses, body_ids, axis=1), resident_rows)
    return (stepped_poses, shifted_poses.reshape(3, BOX_CELLS_X, BOX_CELLS_Y, BOX_CELLS_Z, ATOMS_PER_CELL))
```

```python
import functools

import jax
import jax.numpy as jnp
from jax import lax
from jax.experimental import pallas as pl
from jax.experimental.pallas import tpu as pltpu
from jax.sharding import PartitionSpec as P

MESH = pl.DeviceIdType.MESH
min_reach = 0.15
clash_gain = 20.0
debye_length = 0.5
move_gain = 0.02
turn_gain = 0.01
tiny = 1e-24
log2_e = 1.4426950408889634

STEPS = [(a, b, c) for a in (-1, 0, 1) for b in (-1, 0, 1) for c in (-1, 0, 1)]
HOME = 13
UPPER = range(14, 27)
OTHERS = [code for code in range(27) if code != HOME]
WIDE = 768
f32 = jnp.float32
bf16 = jnp.bfloat16


def three_terms(value):
    high = value.astype(bf16).astype(f32)
    rest = value - high
    middle = rest.astype(bf16).astype(f32)
    return high, middle, rest - middle


def window(block, code):
    dx, dy, dz = STEPS[code]
    return block.at[
        pl.ds(2, 1) if dx == 1 else pl.ds(0, 2),
        {-1: pl.ds(0, 1), 0: pl.ds(1, 2), 1: pl.ds(3, 1)}[dy],
        {-1: pl.ds(0, 1), 0: pl.ds(1, 4), 1: pl.ds(5, 1)}[dz],
    ]


def border(block, code):
    dx, dy, dz = STEPS[code]
    return block.at[
        pl.ds(0, 1) if dx == 1 else pl.ds(0, 2),
        {-1: pl.ds(2, 1), 0: pl.ds(1, 2), 1: pl.ds(1, 1)}[dy],
        {-1: pl.ds(4, 1), 0: pl.ds(1, 4), 1: pl.ds(1, 1)}[dz],
    ]


def extent(code):
    dx, dy, dz = STEPS[code]
    return (1 if dx else 2, 1 if dy else 2, 1 if dz else 4)


def kernel(
    counts,
    local_ref, charge_ref, radius_ref, slot_ref, cell_counts, pose_ref, mobility_ref, noise_ref,
    pose_out, place_out,
    rows_in, rows_new, drive, message, message_new, near, near_new, pick, extended, reply,
    back, arms, column, pull, push, loads, parts, parts_in, sums,
    send_sems, recv_sems,
):
    here = {name: lax.axis_index(name) for name in counts}
    lane = lax.broadcasted_iota(jnp.int32, (8, 128), 1)
    sub = lax.broadcasted_iota(jnp.int32, (8, 128), 0)
    box = [2.0 * counts["gx"], 2.0 * counts["gy"], 4.0 * counts["gz"]]

    def device(code):
        return {
            name: lax.rem(here[name] + (step + counts[name]), counts[name])
            for name, step in zip(("gx", "gy", "gz"), STEPS[code])
        }

    def by_row(values):
        return jnp.where(sub == 0, values[0], jnp.where(sub == 1, values[1], values[2]))

    def copy(source, target, phase, slot, code):
        return pltpu.make_async_remote_copy(
            src_ref=source,
            dst_ref=target,
            send_sem=send_sems.at[phase, slot],
            recv_sem=recv_sems.at[phase, slot],
            device_id=device(code),
            device_id_type=MESH,
        )

    def cell_at(index):
        return index // 8, index // 4 % 2, index % 4

    barrier = pltpu.get_barrier_semaphore()
    for code in OTHERS:
        pl.semaphore_signal(barrier, inc=1, device_id=device(code), device_id_type=MESH)

    def packed(rows, target):
        total = rows[9:17, :]
        total = pltpu.roll(total, 96, 1)
        for group in range(3):
            block = rows[pl.ds(group, 8, stride=3), :]
            total = total + (pltpu.roll(block, 32 * group, 1) if group else block)
        target[...] = total

    rows_in[...] = jnp.zeros_like(rows_in)
    rows_in[0:12, 0:24] = pose_ref[...]
    packed(rows_in, message)
    drive[...] = jnp.zeros_like(drive)
    drive[0:2, 0:24] = mobility_ref[...]
    drive[2:8, 0:24] = noise_ref[...]
    rows_new[...] = jnp.zeros_like(rows_new)

    pl.semaphore_wait(barrier, len(OTHERS))

    def spread(source, target, phase):
        copies = [copy(source, target.at[26 - code], phase, code, code) for code in OTHERS]
        for each in copies:
            each.start()
        return copies

    pose_copies = spread(message, near, 0)
    near[HOME] = message[...]

    def clear_push(index, _):
        push[index] = jnp.zeros((3, 16, 8, 128), f32)
        return 0

    lax.fori_loop(0, 16, clear_push, 0)

    def clear_pull(index, _):
        pull[index // 24, index // 6 % 4, index % 6] = jnp.zeros((3, 8, 128), f32)
        return 0

    lax.fori_loop(0, 72, clear_pull, 0)
    for x in range(2):
        for y in range(2):
            extended[x, y + 1, 0] = jnp.where(sub == 4, -4.0, 0.0)

    body_iota = lax.broadcasted_iota(jnp.int32, (WIDE, 128), 0)

    def build_pick(index, _):
        x, y, z = cell_at(index)
        slots = slot_ref[x, y, pl.ds(z, 1), :]
        pick[:, pl.ds(pl.multiple_of(index * 128, 128), 128)] = jnp.where(
            body_iota == slots, 1.0, 0.0
        ).astype(bf16)
        return 0

    lax.fori_loop(0, 16, build_pick, 0)

    def selector(blocks):
        groups = [[None] * (WIDE // 128) for _ in range(4)]
        for code in range(27):
            block = blocks[code]
            tile, start = divmod(24 * code, 128)
            for group in range(4):
                shift = (start - 32 * group) % 128
                turned = pltpu.roll(block, shift, 1) if shift else block
                pieces = [(tile, (lane >= start) & (lane < start + 24))]
                if start + 24 > 128:
                    pieces.append((tile + 1, lane < start + 24 - 128))
                for at, mask in pieces:
                    held = groups[group][at]
                    groups[group][at] = jnp.where(mask, turned, 0.0 if held is None else held)
        whole = jnp.concatenate([jnp.concatenate(tiles, axis=1) for tiles in groups], axis=0)
        return jnp.concatenate(three_terms(whole), axis=0).astype(bf16)

    def gathered(left, chunk):
        right = pick[:, pl.ds(pl.multiple_of(chunk * 256, 256), 256)]
        out = jnp.dot(left, right, preferred_element_type=f32)
        return out[0:32] + out[32:64] + out[64:96]

    def arm_of(rows, x, y, z):
        total = None
        for axis in range(3):
            term = rows[8 * axis : 8 * axis + 8] * local_ref[axis, x, y, pl.ds(z, 1), :]
            total = term if total is None else total + term
        return total

    for each in pose_copies:
        each.wait_recv()
    left = selector(near)
    middle = [
        2 * here["gx"].astype(f32) + 1.0,
        2 * here["gy"].astype(f32) + 1.0,
        4 * here["gz"].astype(f32) + 2.0,
    ]
    middle_rows = by_row(middle)
    box_rows = by_row(box)

    def place(chunk, _):
        table = gathered(left, chunk)
        for half in range(2):
            index = 2 * chunk + half
            x, y, z = cell_at(index)
            rows = table[:, 128 * half : 128 * half + 128]
            arm = arm_of(rows, x, y, z)
            arms[index] = arm
            at = arm + rows[24:32] - middle_rows
            at = at - box_rows * jnp.floor(at / box_rows + 0.5)
            filled = lane[0:1] < cell_counts[x, y, z]
            charge = jnp.where(filled, charge_ref[x, y, pl.ds(z, 1), :], 0.0)
            radius = jnp.where(filled, radius_ref[x, y, pl.ds(z, 1), :], -4.0)
            at = jnp.where(sub < 3, at, jnp.where(sub == 3, charge, jnp.where(sub == 4, radius, 0.0)))
            extended[x, y + 1, z + 1] = at
            turned = jnp.transpose(at)
            for row in range(5):
                value = turned[:, row : row + 1]
                if row == 3:
                    value = value * (1.0 / clash_gain)
                column[index, row] = jnp.broadcast_to(value, (128, 128)).reshape(16, 8, 128)
        return 0

    lax.fori_loop(0, 8, place, 0)

    halo_copies = [
        copy(border(extended, code), window(extended, code), 1, code, 26 - code) for code in UPPER
    ]
    for each in halo_copies:
        each.start()

    def pairs(index, partners):
        def step(turn, _):
            rows = pl.ds(2 * turn, 2)
            own = [column[index, row, rows] for row in range(5)]
            total = [None] * 3
            for bx, by, bz, both in partners:
                other = [
                    jnp.broadcast_to(extended[bx, by, bz, row : row + 1, :], (8, 128))[None]
                    for row in range(5)
                ]
                delta = [own[axis] - other[axis] for axis in range(3)]
                dist_sq = jnp.maximum(
                    delta[0] * delta[0] + delta[1] * delta[1] + delta[2] * delta[2], tiny
                )
                inverse = lax.rsqrt(dist_sq)
                dist = dist_sq * inverse
                inverse = jnp.minimum(inverse, 1.0 / min_reach)
                fade = jnp.maximum(1.0 - dist_sq, 0.0)
                decay = jnp.exp2(dist * (-log2_e / debye_length))
                clash = jnp.maximum((own[4] + other[4]) - dist, 0.0)
                screened = (
                    ((own[3] * other[3]) * decay)
                    * (fade * fade)
                    * ((inverse + 1.0 / debye_length) * inverse)
                )
                weight = (clash + screened) * inverse
                for axis in range(3):
                    part = weight * delta[axis]
                    total[axis] = part if total[axis] is None else total[axis] + part
                    if both:
                        pull[bx, by, bz, axis] += part[0] + part[1]
            for axis in range(3):
                push[index, axis, rows] += total[axis]
            return 0

        lax.fori_loop(0, 8, step, 0)

    def flat(x, y, z):
        return 8 * x + 4 * y + z

    columns = [(0, 0), (0, 1), (1, 0), (1, 1)]

    def own_pairs(at):
        x, y = columns[at]

        def run(z, last):
            partners = [(x, y + 1, z + 1, False)]
            if not last:
                partners.append((x, y + 1, z + 2, True))
            for bx, by in columns[at + 1 :]:
                for dz in (0, 1) if last else (0, 1, 2):
                    partners.append((bx, by + 1, z + dz, True))
            pairs(flat(x, y, z), partners)

        def lower(z, _):
            run(z, False)
            return 0

        lax.fori_loop(0, 3, lower, 0)
        run(3, True)

    own_pairs(0)

    for each in halo_copies:
        each.wait_recv()
    for code in UPPER:
        dx, dy, dz = STEPS[code]
        offset = by_row([2.0 * dx, 2.0 * dy, 4.0 * dz])
        offset = jnp.where(sub < 3, offset, 0.0)
        region = window(extended, code)
        region[...] = region[...] + offset

    for x, y in columns[1:]:
        shells = [
            (bx, by)
            for bx in range(3)
            for by in range(-1, 3)
            if abs(bx - x) <= 1 and abs(by - y) <= 1 and (bx == 2 or by == 2)
        ]

        def across(z, _):
            pairs(
                flat(x, y, z), [(bx, by + 1, z + dz, True) for bx, by in shells for dz in range(3)]
            )
            return 0

        lax.fori_loop(0, 4, across, 0)

    def upward(at, _):
        pairs(4 * at + 3, [(bx, by + 1, 5, True) for bx, by in columns])
        return 0

    lax.fori_loop(0, 4, upward, 0)

    def pulled(x, y, z):
        total = [jnp.sum(pull[x, y, z, axis], axis=0, keepdims=True) for axis in range(3)]
        return jnp.where(sub < 3, by_row(total), 0.0)

    def reply_cells(count, cell):
        def step(index, _):
            x, y, z = cell(index)
            reply[x, y, z] = pulled(x, y, z)
            return 0

        lax.fori_loop(0, count, step, 0)

    reply_cells(24, lambda i: (2, i // 6, i % 6))
    reply_cells(12, lambda i: (i // 6, 3, i % 6))
    reply_cells(4, lambda i: (i // 2, i % 2 + 1, 5))

    def inbox(code):
        nx, ny, nz = extent(code)
        return back.at[code - 14, pl.ds(0, nx), pl.ds(0, ny), pl.ds(0, nz)]

    reply_copies = [copy(window(reply, code), inbox(code), 2, code, code) for code in UPPER]
    for each in reply_copies:
        each.start()

    for at in range(1, 4):
        own_pairs(at)

    def collect(index, _):
        x, y, z = cell_at(index)
        sums_xyz = [
            jnp.sum(push[index, axis].reshape(128, 128), axis=1, keepdims=True) for axis in range(3)
        ]
        at = lax.broadcasted_iota(jnp.int32, (128, 8), 1)
        stacked = jnp.where(
            at == 0, sums_xyz[0], jnp.where(at == 1, sums_xyz[1], jnp.where(at == 2, sums_xyz[2], 0.0))
        )
        reply[x, y + 1, z + 1] = jnp.transpose(stacked) - pulled(x, y + 1, z + 1)
        return 0

    lax.fori_loop(0, 16, collect, 0)

    for each in reply_copies:
        each.wait_recv()
    for code in UPPER:
        region = border(reply, code)
        region[...] = region[...] - inbox(code)[...]

    def ahead(tile):
        return jnp.where(sub == 2, pltpu.roll(tile, 2, 0), pltpu.roll(tile, 7, 0))

    def load(index, _):
        x, y, z = cell_at(index)
        force = reply[x, y + 1, z + 1] * clash_gain
        force = jnp.where(sub < 3, force, 0.0)
        arm = jnp.where(sub < 3, arms[index], 0.0)
        force_1, arm_1 = ahead(force), ahead(arm)
        torque = arm_1 * ahead(force_1) - ahead(arm_1) * force_1
        torque = jnp.where((sub >= 3) & (sub < 6), pltpu.roll(torque, 3, 0), 0.0)
        loads[:, pl.ds(pl.multiple_of(index * 128, 128), 128)] = force + torque
        return 0

    lax.fori_loop(0, 16, load, 0)
    terms = jnp.concatenate(three_terms(loads[...]), axis=0).astype(bf16)
    by_body = lax.dot_general(
        terms, pick[...], (((1,), (1,)), ((), ())), preferred_element_type=f32
    )
    by_body = by_body[0:8] + by_body[8:16] + by_body[16:24]
    for code in range(27):
        tile, start = divmod(24 * code, 128)
        piece = by_body[:, 128 * tile : 128 * tile + 128]
        if start:
            piece = pltpu.roll(piece, 128 - start, 1)
        if start + 24 > 128:
            after = pltpu.roll(by_body[:, 128 * tile + 128 : 128 * tile + 256], 128 - start, 1)
            piece = jnp.where(lane < 128 - start, piece, after)
        parts[code] = piece
    part_copies = [copy(parts.at[code], parts_in.at[code], 3, code, code) for code in OTHERS]
    for each in part_copies:
        each.start()
    total = parts[HOME]
    for each in part_copies:
        each.wait_recv()
    for code in OTHERS:
        total = total + parts_in[code]
    sums[...] = total

    old = [rows_in[row : row + 1, :] for row in range(12)]
    push_rate, turn_rate = drive[0:1, :], drive[1:2, :]
    kick = [drive[row : row + 1, :] for row in range(2, 8)]
    body = [sums[row : row + 1, :] for row in range(6)]
    valid = lane[0:1] < 24
    new = []
    spin = [0.5 * (turn_gain * turn_rate * body[3 + axis] + kick[3 + axis]) for axis in range(3)]
    spin_sq = spin[0] * spin[0] + spin[1] * spin[1] + spin[2] * spin[2]
    factor = 2.0 / (1.0 + spin_sq)
    skew = [[None, -spin[2], spin[1]], [spin[2], None, -spin[0]], [-spin[1], spin[0], None]]
    for row in range(3):
        line = []
        for col in range(3):
            inner = spin[row] * spin[col]
            if row == col:
                line.append(1.0 + factor * (inner - spin_sq))
            else:
                line.append(factor * (skew[row][col] + inner))
        for col in range(3):
            new.append(line[0] * old[col] + line[1] * old[3 + col] + line[2] * old[6 + col])
    for axis in range(3):
        new.append(old[9 + axis] + move_gain * push_rate * body[axis] + kick[axis])
    for row in range(12):
        rows_new[row : row + 1, :] = jnp.where(valid, new[row], 0.0)
    packed(rows_new, message_new)
    new_copies = spread(message_new, near_new, 4)
    near_new[HOME] = message_new[...]
    pose_out[...] = rows_new[0:12, 0:24]
    for each in pose_copies + halo_copies + reply_copies + part_copies:
        each.wait_send()
    for each in new_copies:
        each.wait_recv()
    left_new = selector(near_new)

    def finish(chunk, _):
        table = gathered(left_new, chunk)
        for half in range(2):
            x, y, z = cell_at(2 * chunk + half)
            rows = table[:, 128 * half : 128 * half + 128]
            at = arm_of(rows, x, y, z) + rows[24:32]
            for axis in range(3):
                place_out[axis, x, y, pl.ds(z, 1), :] = at[axis : axis + 1, :]
        return 0

    lax.fori_loop(0, 8, finish, 0)
    for each in new_copies:
        each.wait_send()


def solution(mesh):
    counts = {name: mesh.shape[name] for name in ("gx", "gy", "gz")}
    placed = (
        P(None, "gx", "gy", "gz", None),
        P("gx", "gy", "gz", None),
        P("gx", "gy", "gz", None),
        P("gx", "gy", "gz", None),
        P("gx", "gy", "gz"),
        P(None, ("gx", "gy", "gz")),
        P(None, ("gx", "gy", "gz")),
        P(None, ("gx", "gy", "gz")),
    )

    def per_device(*arrays):
        body_local, poses = arrays[0], arrays[5]
        vmem = pl.BlockSpec(memory_space=pltpu.VMEM)
        smem = pl.BlockSpec(memory_space=pltpu.SMEM)
        return pl.pallas_call(
            functools.partial(kernel, counts),
            out_shape=(
                jax.ShapeDtypeStruct(poses.shape, f32),
                jax.ShapeDtypeStruct(body_local.shape, f32),
            ),
            in_specs=[vmem, vmem, vmem, vmem, smem, vmem, vmem, vmem],
            out_specs=(vmem, vmem),
            scratch_shapes=[
                pltpu.VMEM((32, 128), f32),
                pltpu.VMEM((32, 128), f32),
                pltpu.VMEM((8, 128), f32),
                pltpu.VMEM((8, 128), f32),
                pltpu.VMEM((8, 128), f32),
                pltpu.VMEM((27, 8, 128), f32),
                pltpu.VMEM((27, 8, 128), f32),
                pltpu.VMEM((WIDE, 2048), bf16),
                pltpu.VMEM((3, 4, 6, 8, 128), f32),
                pltpu.VMEM((3, 4, 6, 8, 128), f32),
                pltpu.VMEM((13, 2, 2, 4, 8, 128), f32),
                pltpu.VMEM((16, 8, 128), f32),
                pltpu.VMEM((16, 5, 16, 8, 128), f32),
                pltpu.VMEM((3, 4, 6, 3, 8, 128), f32),
                pltpu.VMEM((16, 3, 16, 8, 128), f32),
                pltpu.VMEM((8, 2048), f32),
                pltpu.VMEM((27, 8, 128), f32),
                pltpu.VMEM((27, 8, 128), f32),
                pltpu.VMEM((8, 128), f32),
                pltpu.SemaphoreType.DMA((5, 27)),
                pltpu.SemaphoreType.DMA((5, 27)),
            ],
            compiler_params=pltpu.CompilerParams(
                collective_id=0, has_side_effects=True, vmem_limit_bytes=48 * 1024 * 1024
            ),
        )(*arrays)

    return jax.shard_map(
        per_device,
        mesh=mesh,
        in_specs=placed,
        out_specs=(P(None, ("gx", "gy", "gz")), P(None, "gx", "gy", "gz", None)),
        check_vma=False,
    )
```

```python
import functools

import jax
import jax.numpy as jnp
from jax import lax
from jax.experimental import pallas as pl
from jax.experimental.pallas import tpu as pltpu
from jax.sharding import PartitionSpec as P

MESH = pl.DeviceIdType.MESH
min_reach = 0.15
clash_gain = 20.0
debye_length = 0.5
move_gain = 0.02
turn_gain = 0.01
tiny = 1e-24
unit = 1.4426950408889634 / debye_length

charge_gain = 1.0 / (clash_gain * unit)
force_gain = clash_gain / unit

STEPS = [(a, b, c) for a in (-1, 0, 1) for b in (-1, 0, 1) for c in (-1, 0, 1)]
HOME = 13
UPPER = range(14, 27)
OTHERS = sorted((code for code in range(27) if code != HOME), key=lambda code: -sum(map(abs, STEPS[code])))
WIDE = 768
f32 = jnp.float32
bf16 = jnp.bfloat16


def three_terms(value):
    high = value.astype(bf16).astype(f32)
    rest = value - high
    middle = rest.astype(bf16).astype(f32)
    return high, middle, rest - middle


def window(block, code):
    dx, dy, dz = STEPS[code]
    return block.at[
        pl.ds(2, 1) if dx == 1 else pl.ds(0, 2),
        {-1: pl.ds(0, 1), 0: pl.ds(1, 2), 1: pl.ds(3, 1)}[dy],
        {-1: pl.ds(0, 1), 0: pl.ds(1, 4), 1: pl.ds(5, 1)}[dz],
    ]


def border(block, code):
    dx, dy, dz = STEPS[code]
    return block.at[
        pl.ds(0, 1) if dx == 1 else pl.ds(0, 2),
        {-1: pl.ds(2, 1), 0: pl.ds(1, 2), 1: pl.ds(1, 1)}[dy],
        {-1: pl.ds(4, 1), 0: pl.ds(1, 4), 1: pl.ds(1, 1)}[dz],
    ]


def extent(code):
    dx, dy, dz = STEPS[code]
    return (1 if dx else 2, 1 if dy else 2, 1 if dz else 4)


def kernel(
    counts,
    local_in, charge_in, radius_in, slot_in, counts_in, pose_in, mobility_in, noise_in,
    pose_out, place_out,
    local_ref, charge_ref, radius_ref, slot_ref, cell_counts, pose_ref, mobility_ref, noise_ref,
    rows_in, rows_new, drive, message, message_new, near, near_new, pick, extended, reply,
    back, arms, column, pull, push, loads, parts, parts_in, sums,
    load_sems, send_sems, recv_sems,
):
    here = {name: lax.axis_index(name) for name in counts}
    lane = lax.broadcasted_iota(jnp.int32, (8, 128), 1)
    sub = lax.broadcasted_iota(jnp.int32, (8, 128), 0)
    box = [2.0 * counts["gx"], 2.0 * counts["gy"], 4.0 * counts["gz"]]

    def device(code):
        return {
            name: lax.rem(here[name] + (step + counts[name]), counts[name])
            for name, step in zip(("gx", "gy", "gz"), STEPS[code])
        }

    def by_row(values):
        return jnp.where(sub == 0, values[0], jnp.where(sub == 1, values[1], values[2]))

    def copy(source, target, phase, slot, code):
        return pltpu.make_async_remote_copy(
            src_ref=source,
            dst_ref=target,
            send_sem=send_sems.at[phase, slot],
            recv_sem=recv_sems.at[phase, slot],
            device_id=device(code),
            device_id_type=MESH,
        )

    def cell_at(index):
        return index // 8, index // 4 % 2, index % 4

    barrier = pltpu.get_barrier_semaphore()
    for code in OTHERS:
        pl.semaphore_signal(barrier, inc=1, device_id=device(code), device_id_type=MESH)

    fetches = {
        name: pltpu.make_async_copy(source, target, load_sems.at[at])
        for at, (name, source, target) in enumerate(
            [
                ("pose", pose_in, pose_ref),
                ("slot", slot_in, slot_ref),
                ("mobility", mobility_in, mobility_ref),
                ("noise", noise_in, noise_ref),
                ("local", local_in, local_ref),
                ("charge", charge_in, charge_ref),
                ("radius", radius_in, radius_ref),
                ("counts", counts_in, cell_counts),
            ]
        )
    }
    for fetch in fetches.values():
        fetch.start()

    def packed(rows, target):
        total = rows[9:17, :]
        total = pltpu.roll(total, 96, 1)
        for group in range(3):
            block = rows[pl.ds(group, 8, stride=3), :]
            total = total + (pltpu.roll(block, 32 * group, 1) if group else block)
        target[...] = total

    rows_in[...] = jnp.zeros_like(rows_in)
    rows_new[...] = jnp.zeros_like(rows_new)
    drive[...] = jnp.zeros_like(drive)
    fetches["pose"].wait()
    rows_in[0:12, 0:24] = pose_ref[...]
    packed(rows_in, message)

    pl.semaphore_wait(barrier, len(OTHERS))

    def spread(source, target, phase):
        copies = [copy(source, target.at[26 - code], phase, code, code) for code in OTHERS]
        for each in copies:
            each.start()
        return copies

    pose_copies = spread(message, near, 0)
    near[HOME] = message[...]
    for name in ("slot", "mobility", "noise", "local", "charge", "radius", "counts"):
        fetches[name].wait()
    drive[0:2, 0:24] = mobility_ref[...]
    drive[2:8, 0:24] = noise_ref[...]

    def clear_push(index, _):
        push[index] = jnp.zeros((3, 16, 8, 128), f32)
        return 0

    lax.fori_loop(0, 16, clear_push, 0)

    def clear_pull(index, _):
        pull[index // 24, index // 6 % 4, index % 6] = jnp.zeros((3, 8, 128), f32)
        return 0

    lax.fori_loop(0, 72, clear_pull, 0)
    for x in range(2):
        for y in range(2):
            extended[x, y + 1, 0] = jnp.where(sub == 4, -4.0 * unit, 0.0)

    body_iota = lax.broadcasted_iota(jnp.int32, (WIDE, 128), 0)

    def build_pick(index, _):
        x, y, z = cell_at(index)
        slots = slot_ref[x, y, pl.ds(z, 1), :]
        pick[:, pl.ds(pl.multiple_of(index * 128, 128), 128)] = jnp.where(
            body_iota == slots, 1.0, 0.0
        ).astype(bf16)
        return 0

    lax.fori_loop(0, 16, build_pick, 0)

    def selector(blocks):
        groups = [[None] * (WIDE // 128) for _ in range(4)]
        for code in range(27):
            block = blocks[code]
            tile, start = divmod(24 * code, 128)
            for group in range(4):
                shift = (start - 32 * group) % 128
                turned = pltpu.roll(block, shift, 1) if shift else block
                pieces = [(tile, (lane >= start) & (lane < start + 24))]
                if start + 24 > 128:
                    pieces.append((tile + 1, lane < start + 24 - 128))
                for at, mask in pieces:
                    held = groups[group][at]
                    groups[group][at] = jnp.where(mask, turned, 0.0 if held is None else held)
        whole = jnp.concatenate([jnp.concatenate(tiles, axis=1) for tiles in groups], axis=0)
        return jnp.concatenate(three_terms(whole), axis=0).astype(bf16)

    def gathered(left, chunk):
        right = pick[:, pl.ds(pl.multiple_of(chunk * 256, 256), 256)]
        out = jnp.dot(left, right, preferred_element_type=f32)
        return out[0:32] + out[32:64] + out[64:96]

    def arm_of(rows, x, y, z):
        total = None
        for axis in range(3):
            term = rows[8 * axis : 8 * axis + 8] * local_ref[axis, x, y, pl.ds(z, 1), :]
            total = term if total is None else total + term
        return total

    for each in pose_copies:
        each.wait_recv()
    left = selector(near)
    middle = [
        2 * here["gx"].astype(f32) + 1.0,
        2 * here["gy"].astype(f32) + 1.0,
        4 * here["gz"].astype(f32) + 2.0,
    ]
    middle_rows = by_row(middle)
    box_rows = by_row(box)

    def place(chunk, _):
        table = gathered(left, chunk)
        for half in range(2):
            index = 2 * chunk + half
            x, y, z = cell_at(index)
            rows = table[:, 128 * half : 128 * half + 128]
            arm = arm_of(rows, x, y, z)
            arms[index] = arm
            at = arm + rows[24:32] - middle_rows
            at = (at - box_rows * jnp.floor(at / box_rows + 0.5)) * unit
            filled = lane[0:1] < cell_counts[x, y, z]
            radius = radius_ref[x, y, pl.ds(z, 1), :] * unit
            charge = charge_ref[x, y, pl.ds(z, 1), :] * jnp.exp2(-radius)
            charge = jnp.where(filled, charge, 0.0)
            radius = jnp.where(filled, radius, -4.0 * unit)
            at = jnp.where(sub < 3, at, jnp.where(sub == 3, charge, jnp.where(sub == 4, radius, 0.0)))
            extended[x, y + 1, z + 1] = at
            turned = jnp.transpose(at)
            for row in range(5):
                value = turned[:, row : row + 1]
                if row == 3:
                    value = value * charge_gain
                column[index, row] = jnp.broadcast_to(value, (128, 128)).reshape(16, 8, 128)
        return 0

    lax.fori_loop(0, 8, place, 0, unroll=4)

    halo_copies = [
        copy(border(extended, code), window(extended, code), 1, code, 26 - code) for code in UPPER
    ]
    for each in halo_copies:
        each.start()

    def pairs(index, partners):
        def step(turn, _):
            rows = pl.ds(4 * turn, 4)
            own = [column[index, row, rows] for row in range(5)]
            total = [None] * 3
            for bx, by, bz, both in partners:
                other = [
                    jnp.broadcast_to(extended[bx, by, bz, row : row + 1, :], (8, 128))[None]
                    for row in range(5)
                ]
                delta = [own[axis] - other[axis] for axis in range(3)]
                dist_sq = jnp.maximum(
                    delta[0] * delta[0] + delta[1] * delta[1] + delta[2] * delta[2], tiny
                )
                inverse = lax.rsqrt(dist_sq)
                overlap = (own[4] + other[4]) - dist_sq * inverse
                inverse = jnp.minimum(inverse, 1.0 / (min_reach * unit))
                fade = jnp.maximum(unit * unit - dist_sq, 0.0)
                clash = jnp.maximum(overlap, 0.0)
                screened = (
                    ((own[3] * other[3]) * jnp.exp2(overlap))
                    * (fade * fade)
                    * ((inverse + 1.0 / (debye_length * unit)) * inverse)
                )
                weight = (clash + screened) * inverse
                for axis in range(3):
                    part = weight * delta[axis]
                    total[axis] = part if total[axis] is None else total[axis] + part
                    if both:
                        pull[bx, by, bz, axis] += (part[0] + part[1]) + (part[2] + part[3])
            for axis in range(3):
                push[index, axis, rows] += total[axis]
            return 0

        lax.fori_loop(0, 4, step, 0)

    def flat(x, y, z):
        return 8 * x + 4 * y + z

    columns = [(0, 0), (0, 1), (1, 0), (1, 1)]

    def own_pairs(at):
        x, y = columns[at]

        def run(z, last):
            partners = [(x, y + 1, z + 1, False)]
            if not last:
                partners.append((x, y + 1, z + 2, True))
            for bx, by in columns[at + 1 :]:
                for dz in (0, 1) if last else (0, 1, 2):
                    partners.append((bx, by + 1, z + dz, True))
            pairs(flat(x, y, z), partners)

        def lower(z, _):
            run(z, False)
            return 0

        lax.fori_loop(0, 3, lower, 0)
        run(3, True)

    own_pairs(0)

    for each in halo_copies:
        each.wait_recv()
    for code in UPPER:
        dx, dy, dz = STEPS[code]
        offset = by_row([2.0 * unit * dx, 2.0 * unit * dy, 4.0 * unit * dz])
        offset = jnp.where(sub < 3, offset, 0.0)
        region = window(extended, code)
        region[...] = region[...] + offset

    for x, y in columns[1:]:
        shells = [
            (bx, by)
            for bx in range(3)
            for by in range(-1, 3)
            if abs(bx - x) <= 1 and abs(by - y) <= 1 and (bx == 2 or by == 2)
        ]

        def across(z, _):
            pairs(
                flat(x, y, z), [(bx, by + 1, z + dz, True) for bx, by in shells for dz in range(3)]
            )
            return 0

        lax.fori_loop(0, 4, across, 0)

    def upward(at, _):
        pairs(4 * at + 3, [(bx, by + 1, 5, True) for bx, by in columns])
        return 0

    lax.fori_loop(0, 4, upward, 0)

    def pulled(x, y, z):
        total = [jnp.sum(pull[x, y, z, axis], axis=0, keepdims=True) for axis in range(3)]
        return jnp.where(sub < 3, by_row(total), 0.0)

    def reply_cells(count, cell):
        def step(index, _):
            x, y, z = cell(index)
            reply[x, y, z] = pulled(x, y, z)
            return 0

        lax.fori_loop(0, count, step, 0, unroll=4)

    reply_cells(24, lambda i: (2, i // 6, i % 6))
    reply_cells(12, lambda i: (i // 6, 3, i % 6))
    reply_cells(4, lambda i: (i // 2, i % 2 + 1, 5))

    def inbox(code):
        nx, ny, nz = extent(code)
        return back.at[code - 14, pl.ds(0, nx), pl.ds(0, ny), pl.ds(0, nz)]

    reply_copies = [copy(window(reply, code), inbox(code), 2, code, code) for code in UPPER]
    for each in reply_copies:
        each.start()

    for at in range(1, 4):
        own_pairs(at)

    def collect(index, _):
        x, y, z = cell_at(index)
        sums_xyz = [
            jnp.sum(push[index, axis].reshape(128, 128), axis=1, keepdims=True) for axis in range(3)
        ]
        at = lax.broadcasted_iota(jnp.int32, (128, 8), 1)
        stacked = jnp.where(
            at == 0, sums_xyz[0], jnp.where(at == 1, sums_xyz[1], jnp.where(at == 2, sums_xyz[2], 0.0))
        )
        reply[x, y + 1, z + 1] = jnp.transpose(stacked) - pulled(x, y + 1, z + 1)
        return 0

    lax.fori_loop(0, 16, collect, 0, unroll=4)

    for each in reply_copies:
        each.wait_recv()
    for code in UPPER:
        region = border(reply, code)
        region[...] = region[...] - inbox(code)[...]

    def ahead(tile):
        return jnp.where(sub == 2, pltpu.roll(tile, 2, 0), pltpu.roll(tile, 7, 0))

    def load(index, _):
        x, y, z = cell_at(index)
        force = reply[x, y + 1, z + 1] * force_gain
        force = jnp.where(sub < 3, force, 0.0)
        arm = jnp.where(sub < 3, arms[index], 0.0)
        force_1, arm_1 = ahead(force), ahead(arm)
        torque = arm_1 * ahead(force_1) - ahead(arm_1) * force_1
        torque = jnp.where((sub >= 3) & (sub < 6), pltpu.roll(torque, 3, 0), 0.0)
        loads[:, pl.ds(pl.multiple_of(index * 128, 128), 128)] = force + torque
        return 0

    lax.fori_loop(0, 16, load, 0, unroll=8)
    terms = jnp.concatenate(three_terms(loads[...]), axis=0).astype(bf16)
    by_body = lax.dot_general(
        terms, pick[...], (((1,), (1,)), ((), ())), preferred_element_type=f32
    )
    by_body = by_body[0:8] + by_body[8:16] + by_body[16:24]
    for code in range(27):
        tile, start = divmod(24 * code, 128)
        piece = by_body[:, 128 * tile : 128 * tile + 128]
        if start:
            piece = pltpu.roll(piece, 128 - start, 1)
        if start + 24 > 128:
            after = pltpu.roll(by_body[:, 128 * tile + 128 : 128 * tile + 256], 128 - start, 1)
            piece = jnp.where(lane < 128 - start, piece, after)
        parts[code] = piece
    part_copies = [copy(parts.at[code], parts_in.at[code], 3, code, code) for code in OTHERS]
    for each in part_copies:
        each.start()
    total = parts[HOME]
    for each in part_copies:
        each.wait_recv()
    for code in OTHERS:
        total = total + parts_in[code]
    sums[...] = total

    old = [rows_in[row : row + 1, :] for row in range(12)]
    push_rate, turn_rate = drive[0:1, :], drive[1:2, :]
    kick = [drive[row : row + 1, :] for row in range(2, 8)]
    body = [sums[row : row + 1, :] for row in range(6)]
    valid = lane[0:1] < 24
    new = []
    spin = [0.5 * (turn_gain * turn_rate * body[3 + axis] + kick[3 + axis]) for axis in range(3)]
    spin_sq = spin[0] * spin[0] + spin[1] * spin[1] + spin[2] * spin[2]
    factor = 2.0 / (1.0 + spin_sq)
    skew = [[None, -spin[2], spin[1]], [spin[2], None, -spin[0]], [-spin[1], spin[0], None]]
    for row in range(3):
        line = []
        for col in range(3):
            inner = spin[row] * spin[col]
            if row == col:
                line.append(1.0 + factor * (inner - spin_sq))
            else:
                line.append(factor * (skew[row][col] + inner))
        for col in range(3):
            new.append(line[0] * old[col] + line[1] * old[3 + col] + line[2] * old[6 + col])
    for axis in range(3):
        new.append(old[9 + axis] + move_gain * push_rate * body[axis] + kick[axis])
    for row in range(12):
        rows_new[row : row + 1, :] = jnp.where(valid, new[row], 0.0)
    packed(rows_new, message_new)
    new_copies = spread(message_new, near_new, 4)
    near_new[HOME] = message_new[...]
    pose_out[...] = rows_new[0:12, 0:24]
    for each in pose_copies + halo_copies + reply_copies + part_copies:
        each.wait_send()
    for each in new_copies:
        each.wait_recv()
    left_new = selector(near_new)

    def finish(chunk, _):
        table = gathered(left_new, chunk)
        for half in range(2):
            x, y, z = cell_at(2 * chunk + half)
            rows = table[:, 128 * half : 128 * half + 128]
            at = arm_of(rows, x, y, z) + rows[24:32]
            for axis in range(3):
                place_out[axis, x, y, pl.ds(z, 1), :] = at[axis : axis + 1, :]
        return 0

    lax.fori_loop(0, 8, finish, 0, unroll=4)
    for each in new_copies:
        each.wait_send()


def solution(mesh):
    counts = {name: mesh.shape[name] for name in ("gx", "gy", "gz")}
    placed = (
        P(None, "gx", "gy", "gz", None),
        P("gx", "gy", "gz", None),
        P("gx", "gy", "gz", None),
        P("gx", "gy", "gz", None),
        P("gx", "gy", "gz"),
        P(None, ("gx", "gy", "gz")),
        P(None, ("gx", "gy", "gz")),
        P(None, ("gx", "gy", "gz")),
    )

    def per_device(*arrays):
        body_local, poses = arrays[0], arrays[5]
        vmem = pl.BlockSpec(memory_space=pltpu.VMEM)
        held = [pltpu.VMEM(array.shape, array.dtype) for array in arrays]
        held[4] = pltpu.SMEM(arrays[4].shape, arrays[4].dtype)
        return pl.pallas_call(
            functools.partial(kernel, counts),
            out_shape=(
                jax.ShapeDtypeStruct(poses.shape, f32),
                jax.ShapeDtypeStruct(body_local.shape, f32),
            ),
            in_specs=[pl.BlockSpec(memory_space=pltpu.HBM)] * 8,
            out_specs=(vmem, vmem),
            scratch_shapes=held
            + [
                pltpu.VMEM((32, 128), f32),
                pltpu.VMEM((32, 128), f32),
                pltpu.VMEM((8, 128), f32),
                pltpu.VMEM((8, 128), f32),
                pltpu.VMEM((8, 128), f32),
                pltpu.VMEM((27, 8, 128), f32),
                pltpu.VMEM((27, 8, 128), f32),
                pltpu.VMEM((WIDE, 2048), bf16),
                pltpu.VMEM((3, 4, 6, 8, 128), f32),
                pltpu.VMEM((3, 4, 6, 8, 128), f32),
                pltpu.VMEM((13, 2, 2, 4, 8, 128), f32),
                pltpu.VMEM((16, 8, 128), f32),
                pltpu.VMEM((16, 5, 16, 8, 128), f32),
                pltpu.VMEM((3, 4, 6, 3, 8, 128), f32),
                pltpu.VMEM((16, 3, 16, 8, 128), f32),
                pltpu.VMEM((8, 2048), f32),
                pltpu.VMEM((27, 8, 128), f32),
                pltpu.VMEM((27, 8, 128), f32),
                pltpu.VMEM((8, 128), f32),
                pltpu.SemaphoreType.DMA((8,)),
                pltpu.SemaphoreType.DMA((5, 27)),
                pltpu.SemaphoreType.DMA((5, 27)),
            ],
            compiler_params=pltpu.CompilerParams(
                collective_id=0, has_side_effects=True, vmem_limit_bytes=67043328
            ),
        )(*arrays)

    return jax.shard_map(
        per_device,
        mesh=mesh,
        in_specs=placed,
        out_specs=(P(None, ("gx", "gy", "gz")), P(None, "gx", "gy", "gz", None)),
        check_vma=False,
    )
```
